32 devices in a mesh: event: 4 (over z), terrain: 8 (over y, x, core).
Axes of the slice: x: 2, y: 2, z: 4, core: 2. Of those that a mesh axis runs over, the one named last changes fastest.
Arguments:
- level_start: float32 [4, 256, 1024], P('event', 'terrain'), may hold values from -18 to 18
- bed_depth: float32 [256, 1024], P('terrain'), may hold values from 0.5 to 2
- wet_bits: int32 [4, 256, 1024], P('event', 'terrain'), may hold values from 0 to 255
- tile_owner: int32 [2048, 1], P('terrain'), may hold values from 0 to 7; in each aligned block of 256 rows (0 to 255, 256 to 511, ...) at most 48 rows name the same one
- vuln_weight: bfloat16 [128, 256], replicated, may hold values from -0.5 to 0.5
- vuln_bias: float32 [256], replicated, may hold values from -2 to 2
- account_index: int32 [3072, 128], P('terrain'), may hold values from 0 to 1023
- bin_index: int32 [3072, 128], P('terrain'), may hold values from 0 to 255
- exposure_value: bfloat16 [3072, 128], P('terrain'), may hold values from 1 to 10
- deductible: float32 [1024], replicated, may hold values from 0 to 0.8
- limit: float32 [1024], replicated, may hold values from 0.5 to 1.5
Outputs:
- level: float32 [4, 256, 1024], P('event', 'terrain')
- net_loss: bfloat16 [4, 1024, 256], P('event')
- portfolio: float32 [1024, 256], P('terrain')
The draws below stay inside these ranges and needn't reach their ends.
Inputs may be any that keep to these rules, and one draw needn't show every extreme that they name: `tile_owner`: among the 256 tiles of one device no owner is named more than 48 times; in some devices one owner is named exactly 48 times. `wet_bits`: bit s (the value // 2**s, mod 2) is 1 where the cell is wet in substep s. `account_index`: rows of an owner's records that no tile reaches are not read.
All inputs are finite; a program needn't handle non-finite values.
Results may differ from the reference program's by a relative error of at most 0.0004.
The reference program's roundings to bfloat16 on the way (of `pieces` and `ratio`) count: a program that leaves them out, or rounds other values in their place, can miss the bound.
Values may be sent and summed in bfloat16 or wider, within the bound.
A program may use at most 64 MiB of HBM per device.

```python
import math
import jax
import jax.numpy as jnp
import numpy as np
from jax import lax

NY = 1024
TILE = 128
BINS = 256
ACCOUNTS = 1024
SUBSTEPS = 8
GROUPS = 4
ROWS = 256
TILES_DEV = 256
TILES = 2048
CAP = 48
SLOTS = 384
N_TERRAIN = 8


def set_ends(array, stream_key, least, top_value):
    longest = array.shape.index(max(array.shape))
    spots = []
    for shift in (0, 1):
        where = [jax.random.randint(jax.random.fold_in(stream_key, axis), (), 0, length) for axis, length in enumerate(array.shape)]
        where[longest] = (where[longest] + shift) % array.shape[longest]
        spots.append(tuple(where))
    return array.at[spots[0]].set(least).at[spots[1]].set(top_value)


def level_of(stream_key, extent, shards, low, top_value):
    loudness, own = 1.0, jax.random.fold_in(stream_key, 6)
    for dim, shards_of in shards:
        draws = jnp.exp(jax.random.uniform(jax.random.fold_in(own, dim), (shards_of,), jnp.float32, low / len(shards), top_value / len(shards)))
        loudness = loudness * jnp.repeat(draws, extent[dim] // shards_of).reshape([-1 if axis == dim else 1 for axis in range(len(extent))])
    return loudness


def routed_block(stream_key, own, number, rows, count, top, bound, lean):
    order = jax.random.permutation(stream_key, count)
    packed, common = shares(count, rows * top, bound, lean, True), shares(count, rows * top, bound, lean, False)
    places = jnp.arange(count)

    def named(lengths, offset_by):
        used = int((lengths > 0).sum())
        fixed = max(1, used // 4)
        passed = fixed + (places - fixed + offset_by * (used - fixed)) % max(1, count - fixed)
        return jnp.zeros((count,), jnp.int32).at[order[jnp.where(places < fixed, places, passed)]].set(jnp.asarray(lengths, jnp.int32))

    lengths = jnp.where(number % 4 == 0, named(packed, number // 4), named(common, number - number // 4 - 1))
    mixed = jax.random.permutation(jax.random.fold_in(own, 3), count)
    donor, sink = mixed[0:count // 2 * 2:2], mixed[1:count // 2 * 2:2]
    room = jnp.minimum(lengths[donor] - 1, bound - lengths[sink]) // 2
    room = jnp.where((donor == order[0]) | (sink == order[0]) | (lengths[sink] == 0), 0, jnp.maximum(room, 0))
    passed = jax.random.randint(jax.random.fold_in(own, 4), (count // 2,), 0, 1 << 20) % (room + 1)
    lengths = lengths.at[donor].add(-passed).at[sink].add(passed)
    items = jnp.searchsorted(jnp.cumsum(lengths), jnp.arange(rows * top), side="right").astype(jnp.int32)
    table = items.reshape(top, rows).T
    table = table[jax.random.permutation(jax.random.fold_in(own, 1), rows)]
    offset_by = jax.random.randint(jax.random.fold_in(own, 2), (rows, 1), 0, top)
    return jnp.take_along_axis(table, (jnp.arange(top)[None, :] + offset_by) % top, axis=1)


def shares(number_of, total, most, lean, full):
    loads = [(1 << 20) // math.isqrt(grade ** lean) + 1 for grade in range(1, number_of + 1)]
    largest = most if full else min(most, max(-(-total // number_of), total * loads[0] // sum(loads)))
    least = 1 if total - largest >= number_of - 1 else 0
    holding, spare = [largest] + [least] * (number_of - 1), total - largest - least * (number_of - 1)
    while spare > 0:
        candidates = [i for i in range(1, number_of) if holding[i] < largest] or [i for i in range(1, number_of) if holding[i] < most]
        whole, remaining = sum([loads[i] for i in candidates]), spare
        for i in candidates:
            addition = min(most - holding[i], max(1, remaining * loads[i] // whole), spare)
            holding[i] = holding[i] + addition
            spare = spare - addition
    return np.array(holding)


def bell_draw(own_key, shape, width, reach, split=(), held_as=jnp.bfloat16):
    loudness = level_of(own_key, shape, split, -0.22, 0.18) if split else 1.0
    result = jax.random.normal(own_key, shape, jnp.float32) * width * loudness
    return jnp.minimum(jnp.maximum(result, -reach), reach).astype(held_as)


def setup_inputs(seed: int = 0) -> dict:
    splits = jax.random.split(jax.random.key(seed), 12)
    level_start = bell_draw(splits[0], (GROUPS, ROWS, NY), 3.0, 18.0, ((0, 4), (1, 8)), jnp.float32)
    bed_depth = jnp.clip(jnp.exp(math.log(2.0) - 1.3862944 * jax.random.uniform(splits[1], (ROWS, NY), jnp.float32) ** level_of(splits[1], (ROWS, NY), ((0, 8),), -0.2, 0.2)), 0.5, 2.0)
    wet_bits = set_ends(jax.random.randint(splits[2], (GROUPS, ROWS, NY), 0, 2 ** SUBSTEPS), jax.random.fold_in(splits[2], 1), 0, (2 ** SUBSTEPS) - 1).astype(jnp.int32)
    tile_owner_keys = jax.random.split(jax.random.fold_in(splits[3], 1), TILES // TILES_DEV)
    tile_owner_turns = jax.random.permutation(jax.random.fold_in(splits[3], 3), TILES // TILES_DEV)
    tile_owner = jax.vmap(lambda own, number: routed_block(jax.random.fold_in(splits[3], 2), own, number, TILES_DEV, N_TERRAIN, 1, CAP, 2))(tile_owner_keys, tile_owner_turns).reshape((TILES, 1))
    vuln_weight = bell_draw(splits[4], (TILE, BINS), TILE ** -0.5, 0.5)
    vuln_bias = jnp.clip(jax.random.uniform(splits[5], (BINS,), jnp.float32, -2.0, 2.0), -2.0, 2.0)
    account_index = set_ends(jax.random.randint(splits[6], (N_TERRAIN * SLOTS, TILE), 0, ACCOUNTS), jax.random.fold_in(splits[6], 1), 0, ACCOUNTS - 1).astype(jnp.int32)
    bin_index = set_ends(jax.random.randint(splits[7], (N_TERRAIN * SLOTS, TILE), 0, BINS), jax.random.fold_in(splits[7], 1), 0, BINS - 1).astype(jnp.int32)
    exposure_value = jnp.clip(jnp.exp(math.log(10.0) - 2.3025851 * jax.random.uniform(splits[8], (N_TERRAIN * SLOTS, TILE), jnp.float32) ** level_of(splits[8], (N_TERRAIN * SLOTS, TILE), ((0, 8),), -0.2, 0.2)), 1.0, 10.0).astype(jnp.bfloat16)
    deductible = jnp.clip(jax.random.uniform(splits[9], (ACCOUNTS,), jnp.float32, 0.0, 0.8), 0.0, 0.8)
    limit = jnp.clip(jax.random.uniform(splits[10], (ACCOUNTS,), jnp.float32, 0.5, 1.5), 0.5, 1.5)
    return dict(level_start=level_start, bed_depth=bed_depth, wet_bits=wet_bits, tile_owner=tile_owner, vuln_weight=vuln_weight, vuln_bias=vuln_bias, account_index=account_index, bin_index=bin_index, exposure_value=exposure_value, deductible=deductible, limit=limit)


courant = 0.5
gravity = 1.0


def pad_columns(field):
    return jnp.pad(field[:, 1:-1, :], ((0, 0), (0, 0), (1, 1)))


def neighbour_mean(field):
    inner = pad_columns(field)
    return 0.25 * (field[:, 2:, :] + field[:, :-2, :] + inner[:, :, 2:] + inner[:, :, :-2])


def friedrichs_step(level, row_speed, col_speed, bed_depth, wet_factor):
    row_flow = bed_depth * row_speed
    col_flow = pad_columns(bed_depth * col_speed)
    level_pad = pad_columns(level)
    new_level = neighbour_mean(level) - 0.5 * courant * ((row_flow[:, 2:, :] - row_flow[:, :-2, :]) + (col_flow[:, :, 2:] - col_flow[:, :, :-2]))
    new_row = (neighbour_mean(row_speed) - 0.5 * courant * gravity * (level[:, 2:, :] - level[:, :-2, :])) * wet_factor
    new_col = (neighbour_mean(col_speed) - 0.5 * courant * gravity * (level_pad[:, :, 2:] - level_pad[:, :, :-2])) * wet_factor
    return new_level, new_row, new_col


def pad_rows(field):
    return jnp.pad(field, ((0, 0), (1, 1), (0, 0)))


def reference(level_start, bed_depth, wet_bits, tile_owner, vuln_weight, vuln_bias, account_index, bin_index, exposure_value, deductible, limit):
    level = level_start
    row_speed = jnp.zeros_like(level_start)
    col_speed = jnp.zeros_like(level_start)
    bed_pad = jnp.pad(bed_depth, ((1, 1), (0, 0)))
    for step in range(SUBSTEPS):
        wet_factor = ((wet_bits // (2 ** step)) % 2).astype(jnp.float32)
        level, row_speed, col_speed = friedrichs_step(pad_rows(level), pad_rows(row_speed), pad_rows(col_speed), bed_pad, wet_factor)
    pieces = level.astype(jnp.bfloat16).reshape(GROUPS, TILES, TILE)
    owner = tile_owner[:, 0].reshape(N_TERRAIN, TILES_DEV)
    onehot = (owner[:, :, None] == jnp.arange(N_TERRAIN, dtype=jnp.int32)[None, None, :]).astype(jnp.int32)
    rank = jnp.sum((jnp.cumsum(onehot, axis=1) - onehot) * onehot, axis=2)
    source = jnp.arange(N_TERRAIN, dtype=jnp.int32)[:, None]
    record = (owner * SLOTS + source * CAP + rank).reshape(TILES).astype(jnp.int32)
    accounts = account_index[record]
    thresholds = bin_index[record]
    values = exposure_value[record]
    block = math.gcd(TILES, 256)
    bin_range = jnp.arange(BINS, dtype=jnp.int32)

    def group_loss(tiles_group):
        ratio = jax.nn.sigmoid(jnp.dot(tiles_group, vuln_weight, preferred_element_type=jnp.float32) + vuln_bias).astype(jnp.bfloat16)

        def add_block(total, block_id):
            start = (block_id * block).astype(jnp.int32)
            ratio_part = lax.dynamic_slice_in_dim(ratio, start, block, 0).astype(jnp.float32)
            account_part = lax.dynamic_slice_in_dim(accounts, start, block, 0)
            threshold_part = lax.dynamic_slice_in_dim(thresholds, start, block, 0)
            value_part = lax.dynamic_slice_in_dim(values, start, block, 0).astype(jnp.float32)
            inside = (bin_range[None, None, :] >= threshold_part[:, :, None]).astype(jnp.float32)
            weight = value_part[:, :, None] * ratio_part[:, None, :] * inside
            total = total + jax.ops.segment_sum(weight.reshape(-1, BINS), account_part.reshape(-1), num_segments=ACCOUNTS)
            return total, None

        total, _ = lax.scan(add_block, jnp.zeros((ACCOUNTS, BINS), jnp.float32), jnp.arange(TILES // block, dtype=jnp.int32))
        return total

    gross = lax.map(group_loss, pieces)
    scaled = gross * (ACCOUNTS / (ROWS * NY))
    net = jnp.minimum(jnp.maximum(scaled - deductible[None, :, None], 0.0), limit[None, :, None])
    portfolio = jnp.sum(net, axis=0) / GROUPS
    return level, net.astype(jnp.bfloat16), portfolio
```

```python
import functools

import jax
import jax.numpy as jnp
from jax import lax
from jax.experimental import pallas as pl
from jax.experimental.pallas import tpu as pltpu
from jax.sharding import PartitionSpec as P

SUBSTEPS = 8
CHUNK = 8
LOW = 256

courant = 0.5
gravity = 1.0

VMEM = pl.BlockSpec(memory_space=pltpu.VMEM)
SMEM = pl.BlockSpec(memory_space=pltpu.SMEM)
MESH = pl.DeviceIdType.MESH


def exchange_kernel(jobs, *refs):
    count = len(jobs)
    sources, targets, sems = refs[:count], refs[count : 2 * count], refs[2 * count :]
    barrier = pltpu.get_barrier_semaphore()
    greeted = 0
    for axis in dict.fromkeys(axis for axis, _ in jobs):
        size = lax.axis_size(axis)
        me = lax.axis_index(axis)
        for hop in range(1, size):
            pl.semaphore_signal(
                barrier, inc=1, device_id={axis: lax.rem(me + hop, size)}, device_id_type=MESH
            )
        greeted += size - 1
    pl.semaphore_wait(barrier, greeted)
    copies = []
    for job, (axis, spread) in enumerate(jobs):
        source, target = sources[job], targets[job]
        local, sent, received = sems[3 * job : 3 * job + 3]
        size = lax.axis_size(axis)
        me = lax.axis_index(axis)
        for hop in range(1, size):
            peer = lax.rem(me + hop, size)
            copy = pltpu.make_async_remote_copy(
                src_ref=source if spread else source.at[peer],
                dst_ref=target.at[me],
                send_sem=sent.at[hop],
                recv_sem=received.at[hop],
                device_id={axis: peer},
                device_id_type=MESH,
            )
            copy.start()
            copies.append(copy)
        own = pltpu.make_async_copy(source if spread else source.at[me], target.at[me], local)
        own.start()
        copies.append(own)
    for copy in copies:
        copy.wait()


def exchange(arrays, jobs, number):
    shapes, scratch = [], []
    for array, (axis, spread) in zip(arrays, jobs):
        size = lax.axis_size(axis)
        shape = (size,) + array.shape if spread else array.shape
        shapes.append(jax.ShapeDtypeStruct(shape, array.dtype))
        scratch += [
            pltpu.SemaphoreType.DMA,
            pltpu.SemaphoreType.DMA((size,)),
            pltpu.SemaphoreType.DMA((size,)),
        ]
    return pl.pallas_call(
        functools.partial(exchange_kernel, jobs),
        out_shape=shapes,
        in_specs=[VMEM] * len(arrays),
        out_specs=[VMEM] * len(arrays),
        scratch_shapes=scratch,
        compiler_params=pltpu.CompilerParams(collective_id=number, has_side_effects=True),
        name="exchange" + str(number),
    )(*arrays)


def flood_kernel(
    rows, slot_count, capacity, above, here, below, wet_above, wet_here, wet_below,
    owner_row, owner_column, weight, bias, level_out, outgoing_out,
):
    first_row = lax.axis_index("terrain") * rows - SUBSTEPS
    total_rows = rows * lax.axis_size("terrain")
    level = jnp.concatenate([above[0], here[0], below[0]], axis=0)
    bed = jnp.concatenate([above[1], here[1], below[1]], axis=0)
    wet = jnp.concatenate([wet_above[...], wet_here[...], wet_below[...]], axis=0)
    shape = level.shape
    tall, width = shape
    row_id = first_row + lax.broadcasted_iota(jnp.int32, shape, 0)
    column = lax.broadcasted_iota(jnp.int32, shape, 1)
    inside = ((row_id >= 0) & (row_id < total_rows)).astype(jnp.float32)
    not_first = (column > 0).astype(jnp.float32)
    not_last = (column < width - 1).astype(jnp.float32)

    def down(field):
        return pltpu.roll(field, tall - 1, 0)

    def up(field):
        return pltpu.roll(field, 1, 0)

    def right(field):
        return pltpu.roll(field, width - 1, 1) * not_last

    def left(field):
        return pltpu.roll(field, 1, 1) * not_first

    row_speed = jnp.zeros(shape, jnp.float32)
    col_speed = jnp.zeros(shape, jnp.float32)
    for step in range(SUBSTEPS):
        wet_factor = ((wet >> step) & 1).astype(jnp.float32) * inside
        ld, lu, lr, ll = down(level), up(level), right(level), left(level)
        new_level = 0.25 * (ld + lu + lr + ll)
        if step:
            row_flow, col_flow = bed * row_speed, bed * col_speed
            new_level = new_level - 0.5 * courant * (
                down(row_flow) - up(row_flow) + (right(col_flow) - left(col_flow))
            )
            row_mean = 0.25 * (
                down(row_speed) + up(row_speed) + right(row_speed) + left(row_speed)
            )
            col_mean = 0.25 * (
                down(col_speed) + up(col_speed) + right(col_speed) + left(col_speed)
            )
            row_speed = (row_mean - 0.5 * courant * gravity * (ld - lu)) * wet_factor
            col_speed = (col_mean - 0.5 * courant * gravity * (lr - ll)) * wet_factor
        else:
            row_speed = (0.0 - 0.5 * courant * gravity * (ld - lu)) * wet_factor
            col_speed = (0.0 - 0.5 * courant * gravity * (lr - ll)) * wet_factor
        level = new_level * inside
    level = level[SUBSTEPS : SUBSTEPS + rows]
    level_out[...] = level
    tile = weight.shape[0]
    blocks = width // tile
    pieces = jnp.concatenate(
        [level[:, j * tile : (j + 1) * tile] for j in range(blocks)], axis=0
    ).astype(jnp.bfloat16)
    ratio = jax.nn.sigmoid(
        jnp.dot(pieces, weight[...], preferred_element_type=jnp.float32) + bias[...]
    ).astype(jnp.bfloat16)
    tiles = rows * blocks
    along = lax.broadcasted_iota(jnp.int32, (tiles, tiles), 1)
    across = lax.broadcasted_iota(jnp.int32, (tiles, tiles), 0)

    def number(place):
        return (place % rows) * blocks + place // rows

    earlier = (owner_column[...] == owner_row[...]) & (number(across) < number(along))
    rank = jnp.sum(earlier.astype(jnp.float32), axis=0, keepdims=True).astype(jnp.int32)
    place = owner_row[...] * capacity + rank
    slot = lax.broadcasted_iota(jnp.int32, (slot_count, tiles), 0)
    chosen = jnp.where(slot == place, 1.0, 0.0).astype(jnp.bfloat16)
    outgoing_out[...] = jnp.dot(chosen, ratio, preferred_element_type=jnp.float32).astype(
        jnp.bfloat16
    )


def loss_kernel(busy, ratio, account, threshold, value, total, left, right):
    accounts, bins = total.shape
    slots, tile = account.shape
    high_count = accounts // LOW
    total[...] = jnp.zeros(total.shape, jnp.float32)
    sub = 16
    low_id = (
        lax.broadcasted_iota(jnp.int32, (LOW, tile), 0).astype(jnp.float32).astype(jnp.bfloat16)
    )
    bin_id = (
        lax.broadcasted_iota(jnp.int32, (sub, bins), 1).astype(jnp.float32).astype(jnp.bfloat16)
    )
    bin_id = jnp.concatenate([bin_id] * (tile // sub), axis=0)

    def rowed(row, height):
        packed = jnp.broadcast_to(row, (sub, row.shape[1])).astype(jnp.bfloat16)
        return jnp.concatenate([packed] * (height // sub), axis=0)

    def chunk(number, _):
        @pl.when(busy[number] != 0)
        def _():
            first = pl.multiple_of(number * CHUNK, CHUNK)
            accounts_now = account[pl.ds(first, CHUNK), :]
            low = (accounts_now & (LOW - 1)).astype(jnp.float32)
            high = accounts_now // LOW
            values = value[pl.ds(first, CHUNK), :]
            bounds = jnp.transpose(threshold[pl.ds(first, CHUNK), :].astype(jnp.float32))
            ratios = ratio[pl.ds(first, CHUNK), :]
            parts = [jnp.where(high == h, values, 0.0) for h in range(high_count)]
            for i in range(CHUNK):
                cells = slice(i * tile, (i + 1) * tile)
                hit = rowed(low[i : i + 1], LOW) == low_id
                for h in range(high_count):
                    left[h * LOW : (h + 1) * LOW, cells] = jnp.where(
                        hit, rowed(parts[h][i : i + 1], LOW), jnp.zeros((), jnp.bfloat16)
                    )
                bound = jnp.broadcast_to(bounds[:, i : i + 1], (tile, bins)).astype(jnp.bfloat16)
                right[cells, :] = jnp.where(
                    bin_id >= bound, rowed(ratios[i : i + 1], tile), jnp.zeros((), jnp.bfloat16)
                )
            total[...] += jnp.dot(left[...], right[...], preferred_element_type=jnp.float32)

        return 0

    lax.fori_loop(0, slots // CHUNK, chunk, 0)


def per_device(
    level_start,
    bed_depth,
    wet_bits,
    tile_owner,
    vuln_weight,
    vuln_bias,
    account_index,
    bin_index,
    exposure_value,
    deductible,
    limit,
):
    _, rows, width = level_start.shape
    tile_cells, bin_count = vuln_weight.shape
    account_count = deductible.shape[0]
    owners = lax.axis_size("terrain")
    events = lax.axis_size("event")
    slot_count = account_index.shape[0]
    capacity = slot_count // owners
    share_rows = account_count // owners
    blocks = width // tile_cells
    tiles = rows * blocks

    here = jnp.stack([level_start[0], bed_depth])
    wet = wet_bits[0]
    forth = [(i, i + 1) for i in range(owners - 1)]
    back = [(i + 1, i) for i in range(owners - 1)]
    above = lax.ppermute(here[:, rows - SUBSTEPS :], "terrain", forth)
    below = lax.ppermute(here[:, :SUBSTEPS], "terrain", back)
    wet_above = lax.ppermute(wet[rows - SUBSTEPS :], "terrain", forth)
    wet_below = lax.ppermute(wet[:SUBSTEPS], "terrain", back)
    owner = tile_owner[:, 0].reshape(rows, blocks).T.reshape(1, tiles)
    level, outgoing = pl.pallas_call(
        functools.partial(flood_kernel, rows, slot_count, capacity),
        out_shape=(
            jax.ShapeDtypeStruct((rows, width), jnp.float32),
            jax.ShapeDtypeStruct((slot_count, bin_count), jnp.bfloat16),
        ),
        in_specs=[VMEM] * 10,
        out_specs=(VMEM, VMEM),
        name="flood",
    )(
        above, here, below, wet_above, wet, wet_below,
        owner, owner.reshape(tiles, 1), vuln_weight, vuln_bias[None, :],
    )
    outgoing = outgoing.reshape(owners, capacity, bin_count)
    (ratio,) = exchange([outgoing], [("terrain", False)], 1)
    ratio = ratio.reshape(slot_count, bin_count).astype(jnp.float32)
    busy = jnp.any(ratio.reshape(slot_count // CHUNK, -1) != 0, axis=1).astype(jnp.int32)
    total = pl.pallas_call(
        loss_kernel,
        out_shape=jax.ShapeDtypeStruct((account_count, bin_count), jnp.float32),
        in_specs=[SMEM] + [VMEM] * 4,
        out_specs=VMEM,
        scratch_shapes=[
            pltpu.VMEM((account_count, CHUNK * tile_cells), jnp.bfloat16),
            pltpu.VMEM((CHUNK * tile_cells, bin_count), jnp.bfloat16),
        ],
        name="losses",
    )(busy, ratio, account_index, bin_index, exposure_value.astype(jnp.float32))
    (parts,) = exchange(
        [total.reshape(owners, share_rows, bin_count)], [("terrain", False)], 2
    )
    scale = account_count / (rows * width * owners)
    lower = lax.axis_index("terrain") * share_rows
    floor = lax.dynamic_slice_in_dim(deductible, lower, share_rows, 0)[:, None]
    roof = lax.dynamic_slice_in_dim(limit, lower, share_rows, 0)[:, None]
    whole = jnp.sum(parts, axis=0)
    net = jnp.minimum(jnp.maximum(whole * scale - floor, 0.0), roof)
    net_loss, nets = exchange(
        [net.astype(jnp.bfloat16), net], [("terrain", True), ("event", True)], 3
    )
    portfolio = jnp.sum(nets, axis=0) / events
    return (level[None], net_loss.reshape(1, account_count, bin_count), portfolio)


def solution(mesh):
    placed = (
        P("event", "terrain", None),
        P("terrain", None),
        P("event", "terrain", None),
        P("terrain", None),
        P(),
        P(),
        P("terrain", None),
        P("terrain", None),
        P("terrain", None),
        P(),
        P(),
    )
    return jax.shard_map(
        per_device,
        mesh=mesh,
        in_specs=placed,
        out_specs=(P("event", "terrain", None), P("event", None, None), P("terrain", None)),
        check_vma=False,
    )
```
